256 devices in a mesh: dp: 32 (over z, y), ctx: 8 (over x, core).
Axes of the slice: x: 4, y: 4, z: 8, core: 2. Of those that a mesh axis runs over, the one named last changes fastest.
Arguments:
- query_rows: bfloat16 [32768, 2048], P(('dp', 'ctx')), may hold values from -6 to 6
- key_rows: bfloat16 [32768, 2048], P(('dp', 'ctx')), may hold values from -6 to 6
- value_rows: bfloat16 [32768, 2048], P(('dp', 'ctx')), may hold values from -6 to 6
- target: bfloat16 [32768, 1536], P(('dp', 'ctx')), may hold values from -18 to 18
- w_out: bfloat16 [2048, 1536], replicated, may hold values from -0.125 to 0.125
- clip_lengths: int32 [32, 4], P('dp'), may hold values from 1 to 512, 1024 in all within a row
- timesteps: int32 [32, 4], P('dp'), may hold values from 0 to 999
- tile_pattern: int32 [32, 8, 8], P('dp'), may hold values 0 or 1
- tau_prev: float32 [1], replicated, may hold values from 1 to 4
Outputs:
- query_grad: bfloat16 [32768, 2048], P(('dp', 'ctx'))
- key_grad: bfloat16 [32768, 2048], P(('dp', 'ctx'))
- value_grad: bfloat16 [32768, 2048], P(('dp', 'ctx'))
- weight_grad: float32 [2048, 1536], P('ctx', 'dp')
The draws below stay inside these ranges and needn't reach their ends.
Inputs may be any that keep to these rules, and one draw needn't show every extreme that they name: `clip_lengths`: each row of clip lengths sums to 1024, and its largest entry is 512.
All inputs are finite; a program needn't handle non-finite values. No bound on the sum of `tile_pattern` on one device may be relied on, other than what follows from the above.
Results may differ from the reference program's by a relative error of at most 0.019.
Values may be sent and summed in bfloat16 or wider, within the bound.
No kernel may reach another device: no remote copies, remote signals or barrier semaphores. Data moves between devices by JAX's collectives and lax.ppermute only.
A program may use at most 128 MiB of HBM per device.

```python
import math
import jax
import jax.numpy as jnp
import numpy as np
from jax import lax

HEADS = 16
HD = 128
OUT = 1536
CLIPS = 4
TILE = 128
DA = 2048
GROUP = 1024
TOKENS = 32768
NT = 8
N_DP = 32


def drawn_rows(key, salt):
    return jnp.clip(jax.random.normal(jax.random.fold_in(key, salt), (TOKENS, DA), jnp.float32), -6.0, 6.0)


def draw_query_rows(key, part):
    return drawn_rows(key, 11).astype(jnp.bfloat16)


def draw_key_rows(key, part):
    return drawn_rows(key, 12).astype(jnp.bfloat16)


def draw_target(key, part):
    pack_ids = (jnp.arange(TOKENS, dtype=jnp.int32) // GROUP).astype(jnp.float32)
    fraction = pack_ids / max(N_DP - 1, 1)
    base = jnp.clip(jax.random.normal(jax.random.fold_in(key, 22), (TOKENS, OUT), jnp.float32), -6.0, 6.0)
    ramp = 1.0 + 2.0 * fraction
    return (base * ramp[:, None]).astype(jnp.bfloat16)


def with_ends(values, key, least, high):
    longest = values.shape.index(max(values.shape))
    spots = []
    for shift in (0, 1):
        where = [jax.random.randint(jax.random.fold_in(key, axis), (), 0, length) for axis, length in enumerate(values.shape)]
        where[longest] = (where[longest] + shift) % values.shape[longest]
        spots.append(tuple(where))
    return values.at[spots[0]].set(least).at[spots[1]].set(high)


def steps_of(stream_key, shape, cuts, smallest, top_value):
    def one(axis_at, parts):
        draws = jax.random.uniform(jax.random.fold_in(jax.random.fold_in(stream_key, 6), axis_at), (parts,), jnp.float32, smallest / len(cuts), top_value / len(cuts))
        return jnp.repeat(jnp.exp(draws), shape[axis_at] // parts).reshape((-1,) + (1,) * (len(shape) - axis_at - 1))

    level = one(*cuts[0])
    for cut in cuts[1:]:
        level = level * one(*cut)
    return level


def split_up(amount, total, reach, lean):
    loads = [(1 << 20) // math.isqrt(grade ** lean) + 1 for grade in range(2, amount + 1)]
    surplus, given = total - reach - (amount - 1), [1] * (amount - 1)
    while surplus > 0:
        free = [i for i in range(amount - 1) if given[i] < reach]
        whole, remaining = sum([loads[i] for i in free]), surplus
        for i in free:
            extra = min(reach - given[i], max(1, remaining * loads[i] // whole), surplus)
            given[i] = given[i] + extra
            surplus = surplus - extra
    return np.array([reach] + given)


def ragged_sizes(key, amount, total, reach, lean):
    if amount == 2:
        one = jax.random.randint(key, (), max(1, total - reach), min(reach, total - 1) + 1)
        return jnp.stack([one, total - one])
    lengths = jnp.asarray(split_up(amount, total, reach, lean), jnp.int32)
    pairs = (amount - 1) // 2
    source_of, receiver = lengths[1:1 + 2 * pairs:2], lengths[2:2 + 2 * pairs:2]
    room = jnp.minimum(source_of - 1, reach - receiver)
    moved = jax.random.randint(jax.random.fold_in(key, 1), (pairs,), 0, 1 << 20) % (room + 1)
    lengths = lengths.at[1:1 + 2 * pairs:2].set(source_of - moved).at[2:2 + 2 * pairs:2].set(receiver + moved)
    return lengths[jax.random.permutation(jax.random.fold_in(key, 2), amount)]


def noise(stream_key, extent, deviation, reach, pieces=(), held_as=jnp.bfloat16):
    result = deviation * jax.random.normal(stream_key, extent, jnp.float32)
    if pieces:
        result = result * steps_of(stream_key, extent, pieces, -0.22, 0.18)
    return jnp.clip(result, -reach, reach).astype(held_as)


def setup_inputs(seed: int = 0) -> dict:
    splits = jax.random.split(jax.random.key(seed), 10)
    query_rows = draw_query_rows(jax.random.fold_in(splits[9], 71), 0)
    key_rows = draw_key_rows(jax.random.fold_in(splits[9], 71), 0)
    value_rows = noise(splits[2], (TOKENS, DA), 1.0, 6.0, ((0, 256),))
    target = draw_target(jax.random.fold_in(splits[9], 71), 0)
    w_out = noise(splits[4], (DA, OUT), DA ** -0.5, 0.125)
    clip_lengths = jax.vmap(lambda own: ragged_sizes(own, CLIPS, GROUP, GROUP // 2, 2))(jax.random.split(splits[5], N_DP)).reshape((N_DP, CLIPS)).astype(jnp.int32)
    timesteps = with_ends(jax.random.randint(splits[6], (N_DP, CLIPS), 0, 1000), jax.random.fold_in(splits[6], 1), 0, 999).astype(jnp.int32)
    tile_pattern = with_ends((jax.random.randint(splits[7], (N_DP, NT, NT), 0, 2) < 1).astype(jnp.int32), jax.random.fold_in(splits[7], 1), 0, 1)
    tau_prev = jnp.clip(jax.random.uniform(splits[8], (1,), jnp.float32, 1.0, 4.0), 1.0, 4.0)
    return dict(query_rows=query_rows, key_rows=key_rows, value_rows=value_rows, target=target, w_out=w_out, clip_lengths=clip_lengths, timesteps=timesteps, tile_pattern=tile_pattern, tau_prev=tau_prev)


MOMENTUM = 0.9

def clip_index(lengths_row, positions):
    ends = jnp.cumsum(lengths_row)
    return lax.optimization_barrier(jnp.sum((positions[:, None] >= ends[None, :]).astype(jnp.int32), axis=1)).astype(jnp.int32)

def attention_mask(clip_ids, pattern, row_total):
    tiles = row_total // TILE
    tile_ok = jnp.broadcast_to(pattern[:, None, :, None], (tiles, TILE, tiles, TILE)).reshape(row_total, row_total) > 0
    tile_ids = jnp.arange(row_total, dtype=jnp.int32) // TILE
    same_tile = tile_ids[:, None] == tile_ids[None, :]
    return (clip_ids[:, None] == clip_ids[None, :]) & (tile_ok | same_tile)

def head_probs(query_head, key_head, allowed):
    score_scale = 1.0 / math.sqrt(HD)
    scores = lax.dot_general(query_head, key_head, (((1,), (1,)), ((), ())), preferred_element_type=jnp.float32) * score_scale
    scores = jnp.where(allowed, scores, -1e+30)
    row_max = lax.optimization_barrier(jnp.max(scores, axis=1))
    unnorm = jnp.where(allowed, jnp.exp(scores - row_max[:, None]), 0.0)
    row_total = lax.optimization_barrier(jnp.sum(unnorm, axis=1))
    return unnorm / row_total[:, None]

def head_backward(query_head, key_head, value_head, out_head, grad_head, allowed):
    score_scale = 1.0 / math.sqrt(HD)
    probs = head_probs(query_head, key_head, allowed)
    probs_low = probs.astype(jnp.bfloat16)
    value_grad = lax.dot_general(probs_low, grad_head, (((0,), (0,)), ((), ())), preferred_element_type=jnp.float32).astype(jnp.bfloat16)
    prob_grad = lax.dot_general(grad_head, value_head, (((1,), (1,)), ((), ())), preferred_element_type=jnp.float32)
    delta = lax.optimization_barrier(jnp.sum(grad_head.astype(jnp.float32) * out_head.astype(jnp.float32), axis=1))
    score_grad = (probs * (prob_grad - delta[:, None])).astype(jnp.bfloat16)
    query_grad = (jnp.dot(score_grad, key_head, preferred_element_type=jnp.float32) * score_scale).astype(jnp.bfloat16)
    key_grad = (lax.dot_general(score_grad, query_head, (((0,), (0,)), ((), ())), preferred_element_type=jnp.float32) * score_scale).astype(jnp.bfloat16)
    return (query_grad, key_grad, value_grad)

def superloss_weight(clip_loss, tau_now):
    argument = jnp.maximum(-0.3, 0.5 * (clip_loss - tau_now))
    branch = jnp.log1p(argument)
    for sweep in range(5):
        exp_value = jnp.exp(branch)
        branch = branch - (branch * exp_value - argument) / (exp_value * (branch + 1.0))
    return jnp.exp(-branch)

def reference(query_rows, key_rows, value_rows, target, w_out, clip_lengths, timesteps, tile_pattern, tau_prev):
    positions = jnp.arange(GROUP, dtype=jnp.int32)
    clip_all = jax.vmap(lambda lengths_row: clip_index(lengths_row, positions))(clip_lengths)
    query_pack = query_rows.reshape(N_DP, GROUP, DA)
    key_pack = key_rows.reshape(N_DP, GROUP, DA)
    value_pack = value_rows.reshape(N_DP, GROUP, DA)

    def forward(inputs):
        query_one, key_one, value_one, clip_one, pattern_one = inputs
        allowed = attention_mask(clip_one, pattern_one, GROUP)
        head_outs = []
        for head in range(HEADS):
            cols = slice(head * HD, (head + 1) * HD)
            probs = head_probs(query_one[:, cols], key_one[:, cols], allowed)
            head_outs.append(jnp.dot(probs.astype(jnp.bfloat16), value_one[:, cols], preferred_element_type=jnp.float32).astype(jnp.bfloat16))
        return jnp.concatenate(head_outs, axis=1)
    attended = lax.map(forward, (query_pack, key_pack, value_pack, clip_all, tile_pattern)).reshape(TOKENS, DA)
    predicted = jnp.dot(attended, w_out, preferred_element_type=jnp.float32)
    residue = predicted - target.astype(jnp.float32)
    row_squares = lax.optimization_barrier(jnp.sum(residue * residue, axis=1)).reshape(N_DP, GROUP)
    onehot = (clip_all[:, :, None] == jnp.arange(CLIPS, dtype=jnp.int32)[None, None, :]).astype(jnp.float32)
    clip_sq = lax.optimization_barrier(jnp.sum(row_squares[:, :, None] * onehot, axis=1))
    clip_len = clip_lengths.astype(jnp.float32)
    step_weight = 1.0 + timesteps.astype(jnp.float32) / 250.0
    clip_loss = step_weight * clip_sq / (clip_len * OUT)
    loss_mean = jnp.sum(clip_loss) / (N_DP * CLIPS)
    tau_now = MOMENTUM * tau_prev[0] + (1.0 - MOMENTUM) * loss_mean
    confidence = superloss_weight(clip_loss, tau_now)
    clip_scale = confidence * step_weight
    row_scale = lax.optimization_barrier(jnp.sum(onehot * clip_scale[:, None, :], axis=2)).reshape(TOKENS)
    pred_grad = (residue * row_scale[:, None]).astype(jnp.bfloat16)
    weight_grad = lax.dot_general(attended, pred_grad, (((0,), (0,)), ((), ())), preferred_element_type=jnp.float32) * (1.0 / math.sqrt(TOKENS))
    attended_grad = lax.dot_general(pred_grad, w_out, (((1,), (1,)), ((), ())), preferred_element_type=jnp.float32).astype(jnp.bfloat16)

    def backward(inputs):
        query_one, key_one, value_one, out_one, grad_one, clip_one, pattern_one = inputs
        allowed = attention_mask(clip_one, pattern_one, GROUP)
        parts_q, parts_k, parts_v = ([], [], [])
        for head in range(HEADS):
            cols = slice(head * HD, (head + 1) * HD)
            grads = head_backward(query_one[:, cols], key_one[:, cols], value_one[:, cols], out_one[:, cols], grad_one[:, cols], allowed)
            parts_q.append(grads[0])
            parts_k.append(grads[1])
            parts_v.append(grads[2])
        return (jnp.concatenate(parts_q, axis=1), jnp.concatenate(parts_k, axis=1), jnp.concatenate(parts_v, axis=1))
    query_grad, key_grad, value_grad = lax.map(backward, (query_pack, key_pack, value_pack, attended.reshape(N_DP, GROUP, DA), attended_grad.reshape(N_DP, GROUP, DA), clip_all, tile_pattern))
    return (query_grad.reshape(TOKENS, DA), key_grad.reshape(TOKENS, DA), value_grad.reshape(TOKENS, DA), weight_grad)
```

```python
import math

import jax
import jax.numpy as jnp
from jax import lax
from jax.sharding import Mesh
from jax.sharding import PartitionSpec as P

HD = 128
OUT = 1536
CLIPS = 4
TILE = 128
DP = ("dp_0", "dp_1")
DP_CTX = ("dp_0", "dp_1", "ctx")


MOMENTUM = 0.9


def sent_to_all(array, axis):
    copies = jnp.broadcast_to(array, (lax.axis_size(axis), *array.shape))
    return lax.all_to_all(copies, axis, split_axis=0, concat_axis=0, tiled=True)


def over_copies(array, axis):
    return jnp.sum(sent_to_all(array, axis), axis=0)


def shifted(chips, flip, count):
    return [
        (i, ((i // 2 + chips) % (count // 2)) * 2 + ((i % 2) ^ flip)) for i in range(count)
    ]


def gathered_pieces(array, axis):
    count = lax.axis_size(axis)
    chips = count // 2
    place = lax.axis_index(axis)
    pieces = [(0, array)]
    for step in range(1, chips):
        pieces.append((step, lax.ppermute(array, axis, shifted(step, 0, count))))
    everything = []
    for step, piece in pieces:
        source = ((place // 2 + chips - step) % chips) * 2
        everything.append((source + place % 2, piece))
        everything.append(
            (source + 1 - place % 2, lax.ppermute(piece, axis, shifted(0, 1, count)))
        )
    return everything


def clip_index(lengths_row, positions):
    ends = jnp.cumsum(lengths_row)
    return jnp.sum((positions[:, None] >= ends[None, :]).astype(jnp.int32), axis=1)


def attention_mask(clip_ids, pattern, row_total):
    tiles = row_total // TILE
    tile_ok = (
        jnp.broadcast_to(pattern[:, None, :, None], (tiles, TILE, tiles, TILE)).reshape(
            row_total, row_total
        )
        > 0
    )
    tile_ids = jnp.arange(row_total, dtype=jnp.int32) // TILE
    same_tile = tile_ids[:, None] == tile_ids[None, :]
    return (clip_ids[:, None] == clip_ids[None, :]) & (tile_ok | same_tile)


def head_probs(query_head, key_head, allowed):
    score_scale = 1.0 / math.sqrt(HD)
    scores = (
        lax.dot_general(
            query_head, key_head, (((1,), (1,)), ((), ())), preferred_element_type=jnp.float32
        )
        * score_scale
    )
    scores = jnp.where(allowed, scores, -1e30)
    row_max = jnp.max(scores, axis=1)
    unnorm = jnp.where(allowed, jnp.exp(scores - row_max[:, None]), 0.0)
    row_total = jnp.sum(unnorm, axis=1)
    return unnorm / row_total[:, None]


def head_backward(query_head, key_head, value_head, out_head, grad_head, allowed):
    score_scale = 1.0 / math.sqrt(HD)
    probs = head_probs(query_head, key_head, allowed)
    probs_low = probs.astype(jnp.bfloat16)
    value_grad = lax.dot_general(
        probs_low, grad_head, (((0,), (0,)), ((), ())), preferred_element_type=jnp.float32
    ).astype(jnp.bfloat16)
    prob_grad = lax.dot_general(
        grad_head, value_head, (((1,), (1,)), ((), ())), preferred_element_type=jnp.float32
    )
    delta = jnp.sum(grad_head.astype(jnp.float32) * out_head.astype(jnp.float32), axis=1)
    score_grad = (probs * (prob_grad - delta[:, None])).astype(jnp.bfloat16)
    query_grad = (
        jnp.dot(score_grad, key_head, preferred_element_type=jnp.float32) * score_scale
    ).astype(jnp.bfloat16)
    key_grad = (
        lax.dot_general(
            score_grad, query_head, (((0,), (0,)), ((), ())), preferred_element_type=jnp.float32
        )
        * score_scale
    ).astype(jnp.bfloat16)
    return (query_grad, key_grad, value_grad)


def superloss_weight(clip_loss, tau_now):
    argument = jnp.maximum(-0.3, 0.5 * (clip_loss - tau_now))
    branch = jnp.log1p(argument)
    for sweep in range(5):
        exp_value = jnp.exp(branch)
        branch = branch - (branch * exp_value - argument) / (exp_value * (branch + 1.0))
    return jnp.exp(-branch)


def on_device(
    query_rows, key_rows, value_rows, target, w_out, clip_lengths, timesteps, tile_pattern, tau_prev
):
    row_count, features = query_rows.shape
    ctx_count = lax.axis_size("ctx")
    dp_count = lax.axis_size(DP)
    pack_rows = row_count * ctx_count
    ctx_place = lax.axis_index("ctx")
    width_dev = features // ctx_count
    heads_dev = width_dev // HD
    sent = jnp.stack(
        [
            rows.reshape(row_count, ctx_count, width_dev).transpose(1, 0, 2)
            for rows in (query_rows, key_rows, value_rows)
        ],
        axis=1,
    )
    held = lax.all_to_all(sent, "ctx", split_axis=0, concat_axis=0, tiled=True)
    query_head, key_head, value_head = (
        held[:, part].reshape(pack_rows, width_dev) for part in range(3)
    )
    lengths_row = clip_lengths[0]
    clip_pack = clip_index(lengths_row, jnp.arange(pack_rows, dtype=jnp.int32))
    allowed = attention_mask(clip_pack, tile_pattern[0], pack_rows)
    head_outs = []
    for head in range(heads_dev):
        cols = slice(head * HD, (head + 1) * HD)
        probs = head_probs(query_head[:, cols], key_head[:, cols], allowed)
        head_outs.append(
            jnp.dot(
                probs.astype(jnp.bfloat16), value_head[:, cols], preferred_element_type=jnp.float32
            ).astype(jnp.bfloat16)
        )
    out_head = jnp.concatenate(head_outs, axis=1)
    out_rows = lax.all_to_all(out_head, "ctx", split_axis=0, concat_axis=1, tiled=True)
    predicted = jnp.dot(out_rows, w_out, preferred_element_type=jnp.float32)
    residue = predicted - target.astype(jnp.float32)
    residue_low = residue.astype(jnp.bfloat16)

    row_squares = jnp.sum(residue * residue, axis=1)
    positions = ctx_place * row_count + jnp.arange(row_count, dtype=jnp.int32)
    clip_rows = clip_index(lengths_row, positions)
    clip_range = jnp.arange(CLIPS, dtype=jnp.int32)
    onehot = (clip_rows[:, None] == clip_range[None, :]).astype(jnp.float32)
    partial_value = jnp.sum(row_squares[:, None] * onehot, axis=0)
    clip_len = lengths_row.astype(jnp.float32)
    step_weight = 1.0 + timesteps[0].astype(jnp.float32) / 250.0
    clip_sq = over_copies(partial_value, "ctx")
    clip_loss = step_weight * clip_sq / (clip_len * OUT)
    loss_sum = over_copies(jnp.sum(clip_loss), DP)
    loss_mean = loss_sum / (dp_count * CLIPS)
    tau_now = MOMENTUM * tau_prev[0] + (1.0 - MOMENTUM) * loss_mean
    clip_scale = superloss_weight(clip_loss, tau_now) * step_weight
    row_scale = jnp.sum(onehot * clip_scale[None, :], axis=1)
    onehot_pack = (clip_pack[:, None] == clip_range[None, :]).astype(jnp.float32)
    pack_scale = jnp.sum(onehot_pack * clip_scale[None, :], axis=1)
    norm_factor = 1.0 / math.sqrt(pack_rows * dp_count)

    pieces = gathered_pieces(residue_low, "ctx")
    w_block = lax.dynamic_slice_in_dim(w_out, ctx_place * width_dev, width_dev, 0)
    residue_pack = jnp.zeros((pack_rows, OUT), jnp.bfloat16)
    for source, piece in pieces:
        residue_pack = lax.dynamic_update_slice_in_dim(residue_pack, piece, source * row_count, 0)
    grad_head = lax.dot_general(
        residue_pack, w_block, (((1,), (1,)), ((), ())), preferred_element_type=jnp.float32
    ).astype(jnp.bfloat16)
    scaled_out = (out_head.astype(jnp.float32) * (pack_scale * norm_factor)[:, None]).astype(
        jnp.bfloat16
    )
    block_terms = lax.dot_general(
        residue_pack, scaled_out, (((0,), (0,)), ((), ())), preferred_element_type=jnp.float32
    )
    far, near = lax.axis_size(DP[0]), lax.axis_size(DP[1])
    share = OUT // (far * near)
    terms = block_terms.astype(jnp.bfloat16).reshape(far, near, share, width_dev)
    near_terms = lax.all_to_all(
        terms.transpose(1, 0, 2, 3), DP[1], split_axis=0, concat_axis=0, tiled=True
    )
    near_sum = jnp.sum(near_terms.astype(jnp.float32), axis=0).astype(jnp.bfloat16)
    far_terms = lax.all_to_all(near_sum, DP[0], split_axis=0, concat_axis=0, tiled=True)
    weight_grad = jnp.sum(far_terms.astype(jnp.float32), axis=0).T

    parts = []
    for head in range(heads_dev):
        cols = slice(head * HD, (head + 1) * HD)
        parts.append(
            head_backward(
                query_head[:, cols],
                key_head[:, cols],
                value_head[:, cols],
                out_head[:, cols],
                grad_head[:, cols],
                allowed,
            )
        )
    grads = jnp.stack(
        [
            jnp.concatenate([part[which] for part in parts], axis=1).reshape(
                ctx_count, row_count, width_dev
            )
            for which in range(3)
        ],
        axis=1,
    )
    back = lax.all_to_all(grads, "ctx", split_axis=0, concat_axis=0, tiled=True)
    query_back, key_back, value_back = (
        (back[:, which].astype(jnp.float32) * row_scale[None, :, None])
        .astype(jnp.bfloat16)
        .transpose(1, 0, 2)
        .reshape(row_count, features)
        for which in range(3)
    )
    return (query_back, key_back, value_back, weight_grad)


def solution(mesh):
    finer = Mesh(mesh.devices.reshape(8, 4, mesh.shape["ctx"]), ("dp_0", "dp_1", "ctx"))
    return jax.shard_map(
        on_device,
        mesh=finer,
        in_specs=(
            P(DP_CTX, None),
            P(DP_CTX, None),
            P(DP_CTX, None),
            P(DP_CTX, None),
            P(),
            P(DP, None),
            P(DP, None),
            P(DP, None, None),
            P(),
        ),
        out_specs=(P(DP_CTX, None), P(DP_CTX, None), P(DP_CTX, None), P("ctx", DP)),
        check_vma=False,
    )
```

```python
import functools
import math

import jax
import jax.numpy as jnp
from jax import lax
from jax.experimental import pallas as pl
from jax.experimental.pallas import tpu as pltpu
from jax.sharding import Mesh
from jax.sharding import PartitionSpec as P

HD = 128
OUT = 1536
CLIPS = 4
TILE = 128
BLOCK = 256
DP = ("dp_0", "dp_1")
DP_CTX = ("dp_0", "dp_1", "ctx")
F32 = jnp.float32
BF16 = jnp.bfloat16


MOMENTUM = 0.9
SCORE_SCALE = 1.0 / math.sqrt(HD)
NT = (((1,), (1,)), ((), ()))
TN = (((0,), (0,)), ((), ()))
NN = (((1,), (0,)), ((), ()))


def product(left, right, dims):
    return lax.dot_general(left, right, dims, preferred_element_type=F32)


def whole(shape):
    return pl.BlockSpec(shape, lambda *_: (0,) * len(shape))


def by_head(shape):
    return pl.BlockSpec(shape, lambda head, *_: (0,) * (len(shape) - 1) + (head,))


def spread_kernel(query_ref, key_ref, value_ref, sent_ref):
    width = sent_ref.shape[3]
    for which, ref in enumerate((query_ref, key_ref, value_ref)):
        for peer in range(sent_ref.shape[0]):
            sent_ref[peer, which] = ref[:, peer * width : (peer + 1) * width]


def spread(query_rows, key_rows, value_rows, count):
    rows, features = query_rows.shape
    return pl.pallas_call(
        spread_kernel,
        out_shape=jax.ShapeDtypeStruct((count, 3, rows, features // count), BF16),
        name="spread",
    )(query_rows, key_rows, value_rows)


def collect_kernel(back_ref, scale_ref, query_ref, key_ref, value_ref):
    width = back_ref.shape[3]
    scale = jnp.broadcast_to(scale_ref[...], (back_ref.shape[2], width))
    for which, ref in enumerate((query_ref, key_ref, value_ref)):
        for peer in range(back_ref.shape[0]):
            ref[:, peer * width : (peer + 1) * width] = (
                back_ref[peer, which].astype(F32) * scale
            ).astype(BF16)


def collect(back, row_scale):
    count, _, rows, width = back.shape
    return pl.pallas_call(
        collect_kernel,
        out_shape=[jax.ShapeDtypeStruct((rows, count * width), BF16)] * 3,
        name="collect",
    )(back, row_scale[:, None])


def forward_kernel(held_ref, bias_ref, out_ref, probs_ref):
    count, _, rows, _ = held_ref.shape
    pack_rows = count * rows
    key = held_ref[:, 1].reshape(pack_rows, HD)
    value = held_ref[:, 2].reshape(pack_rows, HD)
    tiles = BLOCK // rows

    def step(block, carry):
        cols = pl.ds(pl.multiple_of(block * BLOCK, BLOCK), BLOCK)
        query = held_ref[pl.ds(block * tiles, tiles), 0].reshape(BLOCK, HD)
        scores = product(key, query, NT) * (SCORE_SCALE * math.log2(math.e)) + bias_ref[:, cols]
        top = jnp.max(scores, axis=0, keepdims=True)
        unnorm = jnp.exp2(scores - top)
        total = jnp.sum(unnorm, axis=0, keepdims=True)
        probs = (unnorm * (1.0 / total)).astype(BF16)
        probs_ref[0, :, cols] = probs
        out = product(value, probs, TN).T
        out_ref[pl.ds(block * tiles, tiles)] = out.astype(BF16).reshape(tiles, rows, HD)
        return carry

    lax.fori_loop(0, pack_rows // BLOCK, step, 0)


def forward(held, bias):
    count, _, rows, width = held.shape
    pack_rows = count * rows
    heads = width // HD
    return pl.pallas_call(
        forward_kernel,
        grid=(heads,),
        in_specs=[by_head((count, 3, rows, HD)), whole((pack_rows, pack_rows))],
        out_specs=[
            by_head((count, rows, HD)),
            pl.BlockSpec((1, pack_rows, pack_rows), lambda head: (head, 0, 0)),
        ],
        out_shape=[
            jax.ShapeDtypeStruct((count, rows, width), BF16),
            jax.ShapeDtypeStruct((heads, pack_rows, pack_rows), BF16),
        ],
        name="forward",
    )(held, bias)


def backward_kernel(
    places_ref, held_ref, out_ref, probs_ref, weight_ref, *rest, heads
):
    pieces = rest[:-5]
    grads_ref, residue_ref, grad_ref, delta_ref, score_ref = rest[-5:]
    count, _, rows, _ = held_ref.shape
    pack_rows = count * rows
    tiles = BLOCK // rows
    head = pl.program_id(0)

    @pl.when(head == 0)
    def _():
        for order, piece in enumerate(pieces):
            at = pl.ds(pl.multiple_of(places_ref[1 + order] * rows, rows), rows)
            grad = product(piece[...], weight_ref[...], NT).astype(BF16)
            for which in range(heads):
                grad_ref[which, at] = grad[:, which * HD : (which + 1) * HD]
            residue_ref[at] = piece[...]

    grad_low = grad_ref[head]
    delta = grad_low.astype(F32) * out_ref[...].reshape(pack_rows, HD).astype(F32)
    delta_ref[...] = jnp.broadcast_to(jnp.sum(delta.T, axis=0, keepdims=True), delta_ref.shape)
    query = held_ref[:, 0].reshape(pack_rows, HD)
    key = held_ref[:, 1].reshape(pack_rows, HD)
    value = held_ref[:, 2].reshape(pack_rows, HD)

    def over_queries(block, carry):
        at = pl.ds(pl.multiple_of(block * BLOCK, BLOCK), BLOCK)
        prob_grad = product(value, grad_ref[head, at], NT)
        probs = probs_ref[0, :, at].astype(F32)
        score_grad = (probs * (prob_grad - delta_ref[0:1, at])).astype(BF16)
        score_ref[:, at] = score_grad
        query_grad = (product(key, score_grad, TN) * SCORE_SCALE).T
        grads_ref[pl.ds(block * tiles, tiles), 0] = query_grad.astype(BF16).reshape(
            tiles, rows, HD
        )
        return carry

    lax.fori_loop(0, pack_rows // BLOCK, over_queries, 0)

    def over_keys(block, carry):
        at = pl.ds(pl.multiple_of(block * BLOCK, BLOCK), BLOCK)
        key_grad = product(score_ref[at], query, NN) * SCORE_SCALE
        value_grad = product(probs_ref[0, at], grad_low, NN)
        grads_ref[pl.ds(block * tiles, tiles), 1] = key_grad.astype(BF16).reshape(tiles, rows, HD)
        grads_ref[pl.ds(block * tiles, tiles), 2] = value_grad.astype(BF16).reshape(
            tiles, rows, HD
        )
        return carry

    lax.fori_loop(0, pack_rows // BLOCK, over_keys, 0)


def backward(places, held, out, probs, w_out, pieces):
    count, _, rows, width = held.shape
    pack_rows = count * rows
    heads = width // HD
    return pl.pallas_call(
        functools.partial(backward_kernel, heads=heads),
        grid_spec=pltpu.PrefetchScalarGridSpec(
            num_scalar_prefetch=1,
            grid=(heads,),
            in_specs=[
                by_head((count, 3, rows, HD)),
                by_head((count, rows, HD)),
                pl.BlockSpec((1, pack_rows, pack_rows), lambda head, _: (head, 0, 0)),
                pl.BlockSpec((width, OUT), lambda head, places: (places[0], 0)),
            ]
            + [whole((rows, OUT))] * count,
            out_specs=[by_head((count, 3, rows, HD)), whole((pack_rows, OUT))],
            scratch_shapes=[
                pltpu.VMEM((heads, pack_rows, HD), BF16),
                pltpu.VMEM((8, pack_rows), F32),
                pltpu.VMEM((pack_rows, pack_rows), BF16),
            ],
        ),
        out_shape=[
            jax.ShapeDtypeStruct((count, 3, rows, width), BF16),
            jax.ShapeDtypeStruct((pack_rows, OUT), BF16),
        ],
        name="backward",
    )(places, held, out, probs, w_out, *pieces)


def shifted(chips, flip, count):
    return [
        (i, ((i // 2 + chips) % (count // 2)) * 2 + ((i % 2) ^ flip)) for i in range(count)
    ]


def gathered_pieces(array, axis):
    count = lax.axis_size(axis)
    chips = count // 2
    place = lax.axis_index(axis)
    pieces = [(0, array)]
    for step in range(1, chips):
        pieces.append((step, lax.ppermute(array, axis, shifted(step, 0, count))))
    sources, everything = [], []
    for step, piece in pieces:
        source = ((place // 2 + chips - step) % chips) * 2
        sources += [source + place % 2, source + 1 - place % 2]
        everything += [piece, lax.ppermute(piece, axis, shifted(0, 1, count))]
    return sources, everything


def summed_over(value, axis):
    count = lax.axis_size(axis)
    for bit in range(count.bit_length() - 1):
        value = value + lax.ppermute(value, axis, [(i, i ^ (1 << bit)) for i in range(count)])
    return value


def spread_sum(terms, axis):
    count = lax.axis_size(axis)
    place = lax.axis_index(axis)
    total = lax.dynamic_index_in_dim(terms, place, 1, False)
    for step in range(1, count):
        sent = lax.dynamic_index_in_dim(terms, (place + step) % count, 1, False).astype(BF16)
        total = total + lax.ppermute(
            sent, axis, [(i, (i + step) % count) for i in range(count)]
        ).astype(F32)
    return total


def halved_sum(terms, axis):
    count = lax.axis_size(axis)
    place = lax.axis_index(axis)
    bit = 0
    while terms.shape[0] > 1:
        pairs = terms.reshape(terms.shape[0] // 2, 2, *terms.shape[1:])
        mine = (place >> bit) & 1
        sent = lax.dynamic_index_in_dim(pairs, 1 - mine, 1, False).astype(BF16)
        got = lax.ppermute(sent, axis, [(i, i ^ (1 << bit)) for i in range(count)])
        terms = lax.dynamic_index_in_dim(pairs, mine, 1, False) + got.astype(F32)
        bit += 1
    return terms[0]


def clip_index(lengths_row, positions):
    ends = jnp.cumsum(lengths_row)
    return jnp.sum((positions[:, None] >= ends[None, :]).astype(jnp.int32), axis=1)


def attention_bias(clip_ids, pattern, row_total):
    tiles = row_total // TILE
    tile_ok = (pattern > 0) | (jnp.arange(tiles)[:, None] == jnp.arange(tiles)[None, :])
    wide = jnp.broadcast_to(tile_ok.T[:, None, :, None], (tiles, TILE, tiles, TILE)).reshape(
        row_total, row_total
    )
    return jnp.where((clip_ids[:, None] == clip_ids[None, :]) & wide, 0.0, -1e30).astype(F32)


def superloss_weight(clip_loss, tau_now):
    argument = jnp.maximum(-0.3, 0.5 * (clip_loss - tau_now))
    branch = jnp.log1p(argument)
    for sweep in range(5):
        exp_value = jnp.exp(branch)
        branch = branch - (branch * exp_value - argument) / (exp_value * (branch + 1.0))
    return jnp.exp(-branch)


def on_device(
    query_rows, key_rows, value_rows, target, w_out, clip_lengths, timesteps, tile_pattern, tau_prev
):
    row_count, features = query_rows.shape
    ctx_count = lax.axis_size("ctx")
    dp_count = lax.axis_size(DP)
    pack_rows = row_count * ctx_count
    ctx_place = lax.axis_index("ctx")
    width_dev = features // ctx_count
    sent = spread(query_rows, key_rows, value_rows, ctx_count)
    held = lax.all_to_all(sent, "ctx", split_axis=0, concat_axis=0, tiled=True)
    lengths_row = clip_lengths[0]
    clip_pack = clip_index(lengths_row, jnp.arange(pack_rows, dtype=jnp.int32))
    bias = attention_bias(clip_pack, tile_pattern[0], pack_rows)
    out_head, probs = forward(held, bias)
    out_rows = lax.all_to_all(out_head, "ctx", split_axis=0, concat_axis=0, tiled=True)
    predicted = lax.dot_general(
        out_rows.transpose(1, 0, 2).reshape(row_count, features),
        w_out,
        NN,
        preferred_element_type=F32,
    )
    residue = predicted - target.astype(F32)

    row_squares = jnp.sum(residue * residue, axis=1)
    positions = ctx_place * row_count + jnp.arange(row_count, dtype=jnp.int32)
    clip_rows = clip_index(lengths_row, positions)
    clip_range = jnp.arange(CLIPS, dtype=jnp.int32)
    onehot = (clip_rows[:, None] == clip_range[None, :]).astype(F32)
    partial_value = jnp.sum(row_squares[:, None] * onehot, axis=0)
    clip_len = lengths_row.astype(F32)
    step_weight = 1.0 + timesteps[0].astype(F32) / 250.0
    clip_sq = summed_over(partial_value, "ctx")
    clip_loss = step_weight * clip_sq / (clip_len * OUT)
    loss_sum = summed_over(summed_over(jnp.sum(clip_loss), DP[1]), DP[0])
    loss_mean = loss_sum / (dp_count * CLIPS)
    tau_now = MOMENTUM * tau_prev[0] + (1.0 - MOMENTUM) * loss_mean
    clip_scale = superloss_weight(clip_loss, tau_now) * step_weight
    row_scale = jnp.sum(onehot * clip_scale[None, :], axis=1)
    onehot_pack = (clip_pack[:, None] == clip_range[None, :]).astype(F32)
    pack_scale = jnp.sum(onehot_pack * clip_scale[None, :], axis=1)
    norm_factor = 1.0 / math.sqrt(pack_rows * dp_count)

    sources, pieces = gathered_pieces(residue.astype(BF16), "ctx")
    places = jnp.stack([ctx_place] + sources).astype(jnp.int32)
    grads, residue_pack = backward(places, held, out_head, probs, w_out, pieces)
    back = lax.all_to_all(grads, "ctx", split_axis=0, concat_axis=0, tiled=True)

    scaled_out = (
        out_head.reshape(pack_rows, width_dev).astype(F32) * (pack_scale * norm_factor)[:, None]
    ).astype(BF16)
    block_terms = lax.dot_general(residue_pack, scaled_out, TN, preferred_element_type=F32)
    far, near = lax.axis_size(DP[0]), lax.axis_size(DP[1])
    share = OUT // (far * near)
    near_sum = spread_sum(block_terms.reshape(far, near, share, width_dev), DP[1])
    weight_grad = halved_sum(near_sum, DP[0]).T
    return (*collect(back, row_scale), weight_grad)


def solution(mesh):
    finer = Mesh(mesh.devices.reshape(8, 4, mesh.shape["ctx"]), ("dp_0", "dp_1", "ctx"))
    return jax.shard_map(
        on_device,
        mesh=finer,
        in_specs=(
            P(DP_CTX, None),
            P(DP_CTX, None),
            P(DP_CTX, None),
            P(DP_CTX, None),
            P(),
            P(DP, None),
            P(DP, None),
            P(DP, None, None),
            P(),
        ),
        out_specs=(P(DP_CTX, None), P(DP_CTX, None), P(DP_CTX, None), P("ctx", DP)),
        check_vma=False,
    )
```
